32 devices in a mesh: rows: 8 (over y, x, core), cols: 4 (over z).
Axes of the slice: x: 2, y: 2, z: 4, core: 2. Of those that a mesh axis runs over, the one named last changes fastest.
Arguments:
- guidance: float32 [3, 1024, 12288], P(None, 'rows', 'cols'), may hold values from -8 to 8
- initial: float32 [3, 1024, 12288], P(None, 'rows', 'cols'), may hold values from -6 to 6
- labels: int32 [1024, 12288], P('rows', 'cols'), may hold values from 0 to 5
- dirichlet: int32 [1024, 12288], P('rows', 'cols'), may hold values 0 or 1
Outputs:
- blended: float32 [3, 1024, 12288], P(None, 'rows', 'cols')
- residual: float32 [3, 1024, 12288], P(None, 'rows', 'cols')
The draws below stay inside these ranges and needn't reach their ends.
All inputs are finite; a program needn't handle non-finite values. No bound on the sum of `dirichlet` on one device may be relied on, other than what follows from the above.
Results may differ from the reference program's by a relative error of at most 0.0003.
Values sent between devices are 32-bit elements; how exact they have to be, the bound alone decides.
No kernel may reach another device: no remote copies, remote signals or barrier semaphores. Data moves between devices by JAX's collectives and lax.ppermute only.
A program may use at most 128 MiB of HBM per device.

```python
import jax
import jax.numpy as jnp

CH = 3
ITERS = 3
NR = 1024
NC = 12288


def touch_ends(result, rng, least, largest):
    index_at = [jax.random.randint(jax.random.fold_in(rng, axis), (), 0, length) for axis, length in enumerate(result.shape)]
    widest = result.shape.index(max(result.shape))
    neighbour = index_at[:widest] + [(index_at[widest] + 1) % result.shape[widest]] + index_at[widest + 1:]
    return result.at[tuple(index_at)].set(least).at[tuple(neighbour)].set(largest)


def shard_levels(own_key, dims, split, least, top_value):
    level, own = 1.0, jax.random.fold_in(own_key, 6)
    for dim, shards_of in split:
        steps = jnp.exp(jax.random.uniform(jax.random.fold_in(own, dim), (shards_of,), jnp.float32, least / len(split), top_value / len(split)))
        level = level * jnp.repeat(steps, dims[dim] // shards_of).reshape([-1 if axis == dim else 1 for axis in range(len(dims))])
    return level


def noise(own_key, shape, deviation, reach, pieces=(), dtype=jnp.bfloat16):
    factor_of = shard_levels(own_key, shape, pieces, -0.22, 0.18) if pieces else 1.0
    values = jax.random.normal(own_key, shape, jnp.float32) * deviation * factor_of
    return jnp.minimum(jnp.maximum(values, -reach), reach).astype(dtype)


def setup_inputs(seed: int = 0) -> dict:
    key_of = jax.random.split(jax.random.key(seed), 5)
    guidance = noise(key_of[0], (CH, NR, NC), 1.0, 8.0, ((1, 8), (2, 4)), jnp.float32)
    initial = noise(key_of[1], (CH, NR, NC), 1.0, 6.0, ((1, 8), (2, 4)), jnp.float32)
    labels = touch_ends(jax.random.randint(key_of[2], (NR, NC), 0, 6), jax.random.fold_in(key_of[2], 1), 0, 5).astype(jnp.int32)
    dirichlet = touch_ends((jax.random.randint(key_of[3], (NR, NC), 0, 8) < 1).astype(jnp.int32), jax.random.fold_in(key_of[3], 1), 0, 1)
    return dict(guidance=guidance, initial=initial, labels=labels, dirichlet=dirichlet)


SCREEN = 0.1
SEAM_WEIGHT = 0.5


def edge_weights(labels):
    padded = jnp.pad(labels + 1, 1)
    center = padded[1:-1, 1:-1]
    sides = [padded[2:, 1:-1], padded[:-2, 1:-1], padded[1:-1, 2:], padded[1:-1, :-2]]
    return [jnp.where(side == center, 1.0, SEAM_WEIGHT).astype(jnp.float32) for side in sides]


def operate(field, weights):
    padded = jnp.pad(field, ((0, 0), (1, 1), (1, 1)))
    sides = [padded[:, 2:, 1:-1], padded[:, :-2, 1:-1], padded[:, 1:-1, 2:], padded[:, 1:-1, :-2]]
    total = SCREEN * field
    for weight, side in zip(weights, sides):
        total = total + weight * (field - side)
    return total


def reference(guidance, initial, labels, dirichlet):
    free_cells = (1 - dirichlet).astype(jnp.float32)
    weights = edge_weights(labels)
    residual = free_cells * (guidance - operate(initial, weights))
    blended = initial
    direction = residual
    norm_now = jnp.sum(residual * residual, axis=(1, 2))
    for turn_index in range(ITERS):
        applied = free_cells * operate(direction, weights)
        step_size = norm_now / jnp.sum(direction * applied, axis=(1, 2))
        blended = blended + step_size[:, None, None] * direction
        residual = residual - step_size[:, None, None] * applied
        norm_next = jnp.sum(residual * residual, axis=(1, 2))
        direction = residual + (norm_next / norm_now)[:, None, None] * direction
        norm_now = norm_next
    return blended, residual
```

```python
import functools

import jax
import jax.numpy as jnp
from jax import lax
from jax.experimental import pallas as pl
from jax.experimental.pallas import tpu as pltpu
from jax.sharding import PartitionSpec as P

ITERS = 3
SCREEN = 0.1
SEAM_WEIGHT = 0.5

RIM = ITERS + 1
MOMENTS = 2 * ITERS
LANES = 128
SUBS = 8
HEAD = SUBS


def lane_ids(shape):
    return lax.broadcasted_iota(jnp.int32, shape, len(shape) - 1)


def sub_ids(shape):
    return lax.broadcasted_iota(jnp.int32, shape, len(shape) - 2)


def lane_roll(x, shift):
    shift = shift % LANES
    return pltpu.roll(x, shift, x.ndim - 1) if shift else x


def sub_swap(x):
    return pltpu.roll(x, SUBS // 2, x.ndim - 2)


def pack_cols_kernel(guid, init, lab, dirc, to_left, to_right, gb, xb, lb, db, sem):
    tiles = guid.shape[2] // LANES
    copies = []
    for side, tile in enumerate((0, tiles - 1)):
        at = pl.ds(tile * LANES, LANES)
        copies += [
            pltpu.make_async_copy(init.at[:, :, at], xb.at[side], sem.at[side, 0]),
            pltpu.make_async_copy(guid.at[:, :, at], gb.at[side], sem.at[side, 1]),
            pltpu.make_async_copy(lab.at[:, at], lb.at[side], sem.at[side, 2]),
            pltpu.make_async_copy(dirc.at[:, at], db.at[side], sem.at[side, 3]),
        ]
    for copy in copies:
        copy.start()
    for copy in copies:
        copy.wait()
    ch, rows = guid.shape[0], guid.shape[1]

    def block(b, _):
        at = pl.ds(pl.multiple_of(b * SUBS, SUBS), SUBS)
        lane = lane_ids((SUBS, LANES))
        for side, out in ((0, to_left), (1, to_right)):
            fields = [xb[side, c, at, :] for c in range(ch)] + [gb[side, c, at, :] for c in range(ch)]
            fields += [(lb[side, at, :] + 1).astype(jnp.float32), (1 - db[side, at, :]).astype(jnp.float32)]
            packed = jnp.zeros((SUBS, LANES), jnp.float32)
            for i, field in enumerate(fields):
                moved = lane_roll(field, RIM * i if side == 0 else RIM * i + RIM)
                packed = jnp.where((lane >= RIM * i) & (lane < RIM * (i + 1)), moved, packed)
            out[at, :] = packed
        return 0

    lax.fori_loop(0, rows // SUBS, block, 0)


def rim_tile(from_left, from_right, i):
    lane = lane_ids(from_left.shape)
    right = lane_roll(from_right, -RIM * i)
    left = lane_roll(from_left, LANES - RIM - RIM * i)
    return jnp.where(lane < RIM, right, jnp.where(lane >= LANES - RIM, left, 0.0))


def pack_rows_kernel(guid, init, lab, dirc, from_left, from_right, to_up, to_down, gb, xb, lb, db, sem):
    ch, rows = guid.shape[0], guid.shape[1]
    tiles = guid.shape[2] // LANES
    copies = []
    for side, row in enumerate((0, rows - SUBS)):
        at = pl.ds(row, SUBS)
        copies += [
            pltpu.make_async_copy(init.at[:, at, :], xb.at[side], sem.at[side, 0]),
            pltpu.make_async_copy(guid.at[:, at, :], gb.at[side], sem.at[side, 1]),
            pltpu.make_async_copy(lab.at[at, :], lb.at[side], sem.at[side, 2]),
            pltpu.make_async_copy(dirc.at[at, :], db.at[side], sem.at[side, 3]),
        ]
    for copy in copies:
        copy.start()
    for copy in copies:
        copy.wait()
    sub = sub_ids((SUBS, LANES))

    def put(t, side, fields):
        out = (to_up, to_down)[side]
        for j in range(len(fields) // 2):
            one, two = fields[2 * j], sub_swap(fields[2 * j + 1])
            keep = sub < RIM if side == 0 else sub >= SUBS - RIM
            out[j, t] = jnp.where(keep, one, two)

    def tile(t, _):
        at = pl.ds(pl.multiple_of(t * LANES, LANES), LANES)
        for side in range(2):
            fields = [xb[side, c, :, at] for c in range(ch)] + [gb[side, c, :, at] for c in range(ch)]
            fields += [(lb[side, :, at] + 1).astype(jnp.float32), (1 - db[side, :, at]).astype(jnp.float32)]
            put(t, side, fields)
        return 0

    lax.fori_loop(0, tiles, tile, 0)
    for side, row in enumerate((0, rows - SUBS)):
        left, right = from_left[row : row + SUBS, :], from_right[row : row + SUBS, :]
        put(tiles, side, [rim_tile(left, right, i) for i in range(2 * ch + 2)])


def krylov_kernel(
    guid, init, lab, dirc, from_left, from_right, from_up, from_down, xs, v0, v1, v2, v3, out,
    lb, fb, cc, cn, cs, ce, cw, acc, sem,
):
    ch, rows = guid.shape[0], guid.shape[1]
    tiles = guid.shape[2] // LANES
    blocks = rows // SUBS
    group = next(g for g in (6, 5, 4, 3, 2, 1) if tiles % g == 0)
    lane = lane_ids((SUBS, LANES))
    sub = sub_ids((SUBS, LANES))

    def fetch(t):
        src = pl.ds(pl.multiple_of(t * LANES, LANES), LANES)
        dst = pl.ds(HEAD, rows)
        return (
            pltpu.make_async_copy(init.at[:, :, src], xs.at[:, t, dst, :], sem.at[0, t]),
            pltpu.make_async_copy(guid.at[:, :, src], v0.at[:, t, dst, :], sem.at[1, t]),
            pltpu.make_async_copy(lab.at[:, src], lb.at[t, dst, :], sem.at[2, t]),
            pltpu.make_async_copy(dirc.at[:, src], fb.at[t, dst, :], sem.at[3, t]),
        )

    def start(t, _):
        for copy in fetch(t):
            copy.start()
        return 0

    def finish(t, _):
        for copy in fetch(t):
            copy.wait()
        return 0

    lax.fori_loop(0, tiles, start, 0)

    def rim_columns(b, _):
        at = pl.ds(pl.multiple_of(b * SUBS, SUBS), SUBS)
        to = pl.ds(pl.multiple_of(b * SUBS + HEAD, SUBS), SUBS)
        left, right = from_left[at, :], from_right[at, :]
        for c in range(ch):
            xs[c, tiles, to, :] = rim_tile(left, right, c)
            v0[c, tiles, to, :] = rim_tile(left, right, ch + c)
        lb[tiles, to, :] = rim_tile(left, right, 2 * ch).astype(jnp.int32) - 1
        fb[tiles, to, :] = 1 - rim_tile(left, right, 2 * ch + 1).astype(jnp.int32)
        return 0

    lax.fori_loop(0, blocks, rim_columns, 0)
    last = HEAD + rows

    def rim_rows(t, _):
        fields = []
        for j in range(ch + 1):
            up, down = from_up[j, t], from_down[j, t]
            fields.append(jnp.where(sub < RIM, down, up))
            fields.append(sub_swap(jnp.where(sub < RIM, up, down)))
        for to in (0, last):
            to = pl.ds(to, SUBS)
            for c in range(ch):
                xs[c, t, to, :] = fields[c]
                v0[c, t, to, :] = fields[ch + c]
            lb[t, to, :] = fields[2 * ch].astype(jnp.int32) - 1
            fb[t, to, :] = 1 - fields[2 * ch + 1].astype(jnp.int32)
        return 0

    lax.fori_loop(0, tiles + 1, rim_rows, 0)

    def beside(get, t0, n):
        ring = tiles + 1
        first = jnp.where(t0 == 0, ring - 1, t0 - 1)
        after = jnp.where(t0 + n == ring, 0, t0 + n)
        return [get(first)] + [get(t0 + i) for i in range(n)] + [get(after)]

    def east(mid, nxt):
        return lane_roll(jnp.where(lane == 0, nxt, mid), -1)

    def west(prev, mid):
        return lane_roll(jnp.where(lane == LANES - 1, prev, mid), 1)

    def north_south(get, row, rim):
        north, south = get(row - 1, SUBS), get(row + 1, SUBS)
        if rim:
            south = jnp.where(sub == SUBS - 1, get(HEAD, 1), south)
        return north, south

    def weigh(t0, n, row, rim):
        at = pl.ds(row, SUBS)
        ring = beside(lambda t: lb[t, at, :], t0, n)
        for i in range(n):
            t = t0 + i
            mid = ring[i + 1]
            north, south = north_south(lambda r, k, t=t: lb[t, pl.ds(r, k), :], row, rim)
            free = (1 - fb[t, at, :]).astype(jnp.float32)
            half = free * SEAM_WEIGHT
            wn, ws, we, ww = (
                jnp.where(side == mid, free, half)
                for side in (north, south, east(mid, ring[i + 2]), west(ring[i], mid))
            )
            cn[t, at, :], cs[t, at, :], ce[t, at, :], cw[t, at, :] = wn, ws, we, ww
            cc[t, at, :] = free * SCREEN + ((wn + ws) + (we + ww))
            for c in range(ch):
                v0[c, t, at, :] = free * v0[c, t, at, :]

    def apply(src, dst, t0, n, row, rim, sums, minus):
        at = pl.ds(row, SUBS)
        fresh = [[], []]
        for c in range(ch):
            ring = beside(lambda t, c=c: src[c, t, at, :], t0, n)
            squares, products = [], []
            for i in range(n):
                t = t0 + i
                mid = ring[i + 1]
                north, south = north_south(lambda r, k, t=t: src[c, t, pl.ds(r, k), :], row, rim)
                value = cc[t, at, :] * mid - (
                    (cn[t, at, :] * north + cs[t, at, :] * south)
                    + (ce[t, at, :] * east(mid, ring[i + 2]) + cw[t, at, :] * west(ring[i], mid))
                )
                if minus:
                    value = dst[c, t, at, :] - value
                dst[c, t, at, :] = value
                if rim:
                    dst[c, t, 0:SUBS, :] = value
                if sums is not None:
                    squares.append(mid * mid)
                    products.append(mid * value)
            if sums is not None:
                fresh[0].append(functools.reduce(jnp.add, squares))
                fresh[1].append(functools.reduce(jnp.add, products))
        if sums is not None:
            return tuple(s + f for s, f in zip(sums, fresh[0] + fresh[1]))

    def inner(run, carry, wait):
        def column(k, carry):
            if wait:
                lax.fori_loop(jnp.where(k == 0, 0, k * group + 1), jnp.minimum(k * group + group + 1, tiles), finish, 0)

            def body(b, carry):
                return run(k * group, group, pl.multiple_of(b * SUBS + HEAD, SUBS), False, carry)

            return lax.fori_loop(0, blocks, body, carry)

        return lax.fori_loop(0, tiles // group, column, carry)

    def outer(run):
        def column(b, _):
            run(tiles, 1, pl.multiple_of(b * SUBS + HEAD, SUBS), False, None)
            return 0

        def line(t, _):
            run(t, 1, last, True, None)
            return 0

        lax.fori_loop(0, blocks, column, 0)
        lax.fori_loop(0, tiles + 1, line, 0)

    def run_weigh(t0, n, row, rim, carry):
        weigh(t0, n, row, rim)
        return 0

    inner(run_weigh, 0, True)
    outer(run_weigh)

    def run_first(t0, n, row, rim, carry):
        apply(xs, v0, t0, n, row, rim, None, True)
        return 0

    inner(run_first, 0, False)
    outer(run_first)

    zero = jnp.zeros((SUBS, LANES), jnp.float32)
    chain = (v0, v1, v2, v3)
    for s in range(ITERS):
        def run(t0, n, row, rim, carry, s=s):
            return apply(chain[s], chain[s + 1], t0, n, row, rim, carry, False)

        sums = inner(run, (zero,) * (2 * ch), False)
        for i in range(2 * ch):
            acc[2 * ch * s + i] = sums[i]
        if s + 1 < ITERS:
            outer(run)

    count = MOMENTS * ch
    row = jnp.sum(acc[...], axis=1)
    high, low = row, jnp.zeros_like(row)
    for step in (64, 32, 16, 8, 4, 2, 1):
        high, low = pair_add((high, low), (lane_roll(high, step), lane_roll(low, step)))
    ids = sub_ids((count, LANES))
    lanes = lane_ids((count, LANES))
    row = jnp.sum(jnp.where(lanes == ids, high, jnp.where(lanes == ids + LANES // 2, low, 0.0)), axis=0, keepdims=True)
    out[...] = jnp.broadcast_to(row[None], out.shape)


def two_sum(a, b):
    s = a + b
    t = s - a
    return s, (a - (s - t)) + (b - t)


def quick_sum(a, b):
    s = a + b
    return s, b - (s - a)


def halves(a):
    t = 4097.0 * a
    high = t - (t - a)
    return high, a - high


def two_product(a, b):
    p = a * b
    ah, al = halves(a)
    bh, bl = halves(b)
    return p, ((ah * bh - p) + ah * bl + al * bh) + al * bl


def pair_add(a, b):
    s, e = two_sum(a[0], b[0])
    return quick_sum(s, e + (a[1] + b[1]))


def pair_sub(a, b):
    return pair_add(a, (-b[0], -b[1]))


def pair_mul(a, b):
    p, e = two_product(a[0], b[0])
    return quick_sum(p, e + (a[0] * b[1] + a[1] * b[0]))


def pair_scale(a, b):
    p, e = two_product(a[0], b)
    return quick_sum(p, e + a[1] * b)


def galerkin(m):
    scale = 1.0 / m[0][0]
    m = [pair_scale(each, scale) for each in m]

    def minor(a, b, c, d):
        return pair_sub(pair_mul(a, b), pair_mul(c, d))

    d = minor(m[1], m[3], m[2], m[2])
    t = minor(m[1], m[4], m[2], m[3])
    e = minor(m[1], m[5], m[3], m[3])
    z1 = minor(m[1], m[1], m[0], m[2])
    z2 = minor(m[1], m[2], m[0], m[3])
    det = minor(d, e, t, t)[0]
    y2 = minor(d, z2, t, z1)[0] / det
    y1 = minor(e, z1, t, z2)[0] / det
    flat = d[0] <= 1e-11 * (m[1][0] * m[3][0])
    done = flat | (det <= 1e-11 * (d[0] * e[0]))
    y2 = jnp.where(done, 0.0, y2)
    y1 = jnp.where(flat, 0.0, jnp.where(done, z1[0] / d[0], y1))
    rest = pair_sub(m[0], pair_add(pair_scale(m[2], y1), pair_scale(m[3], y2)))
    return rest[0] / m[1][0], y1, y2


def finish_kernel(parts, xs, v0, v1, v2, v3, blended, residual, bb, rb, sem):
    ch, rows = blended.shape[0], blended.shape[1]
    tiles = blended.shape[2] // LANES
    blocks = rows // SUBS
    high = parts[:, 0, :]
    low = lane_roll(high, LANES // 2)
    total = (high, low)
    n = high.shape[0]
    while n > 1:
        n //= 2
        total = pair_add((total[0][:n], total[1][:n]), (total[0][n:], total[1][n:]))
    m = [(lane_roll(total[0], -ch * k), lane_roll(total[1], -ch * k)) for k in range(MOMENTS)]
    y = galerkin(m)
    lanes = lane_ids((1, LANES))
    coef = [
        [jnp.broadcast_to(jnp.sum(jnp.where(lanes == c, each, 0.0), axis=1, keepdims=True), (SUBS, LANES)) for each in y]
        for c in range(ch)
    ]

    def put(t):
        dst = pl.ds(pl.multiple_of(t * LANES, LANES), LANES)
        return (
            pltpu.make_async_copy(bb.at[:, t], blended.at[:, :, dst], sem.at[0, t]),
            pltpu.make_async_copy(rb.at[:, t], residual.at[:, :, dst], sem.at[1, t]),
        )

    def tile(t, _):
        for b in range(blocks):
            at = pl.ds(HEAD + b * SUBS, SUBS)
            to = pl.ds(b * SUBS, SUBS)
            for c in range(ch):
                y0, y1, y2 = coef[c]
                a, p, q, r = v0[c, t, at, :], v1[c, t, at, :], v2[c, t, at, :], v3[c, t, at, :]
                bb[c, t, to, :] = xs[c, t, at, :] + (y0 * a + (y1 * p + y2 * q))
                rb[c, t, to, :] = a - (y0 * p + (y1 * q + y2 * r))
        for copy in put(t):
            copy.start()
        return 0

    def drain(t, _):
        for copy in put(t):
            copy.wait()
        return 0

    lax.fori_loop(0, tiles, tile, 0)
    lax.fori_loop(0, tiles, drain, 0)


ANY = pl.BlockSpec(memory_space=pl.ANY)
VMEM = pl.BlockSpec(memory_space=pltpu.VMEM)


def swap_rims(first, last, axis):
    count = lax.axis_size(axis)
    before = lax.ppermute(last, axis, [(i, i + 1) for i in range(count - 1)])
    after = lax.ppermute(first, axis, [(i + 1, i) for i in range(count - 1)])
    return before, after


def on_device(guidance, initial, labels, dirichlet):
    ch, rows, cols = guidance.shape
    tiles = cols // LANES
    fields = 2 * ch + 2
    f32, i32 = jnp.float32, jnp.int32
    devices = lax.axis_size("rows") * lax.axis_size("cols")

    to_left, to_right = pl.pallas_call(
        pack_cols_kernel,
        out_shape=[jax.ShapeDtypeStruct((rows, LANES), f32)] * 2,
        in_specs=[ANY] * 4,
        out_specs=[VMEM] * 2,
        scratch_shapes=[
            pltpu.VMEM((2, ch, rows, LANES), f32),
            pltpu.VMEM((2, ch, rows, LANES), f32),
            pltpu.VMEM((2, rows, LANES), i32),
            pltpu.VMEM((2, rows, LANES), i32),
            pltpu.SemaphoreType.DMA((2, 4)),
        ],
        name="pack_cols",
    )(guidance, initial, labels, dirichlet)
    from_left, from_right = swap_rims(to_left, to_right, "cols")

    to_up, to_down = pl.pallas_call(
        pack_rows_kernel,
        out_shape=[jax.ShapeDtypeStruct((fields // 2, tiles + 1, SUBS, LANES), f32)] * 2,
        in_specs=[ANY] * 4 + [VMEM] * 2,
        out_specs=[VMEM] * 2,
        scratch_shapes=[
            pltpu.VMEM((2, ch, SUBS, cols), f32),
            pltpu.VMEM((2, ch, SUBS, cols), f32),
            pltpu.VMEM((2, SUBS, cols), i32),
            pltpu.VMEM((2, SUBS, cols), i32),
            pltpu.SemaphoreType.DMA((2, 4)),
        ],
        name="pack_rows",
    )(guidance, initial, labels, dirichlet, from_left, from_right)
    from_up, from_down = swap_rims(to_up, to_down, "rows")

    deep = HEAD + rows + 2 * SUBS
    field = pltpu.VMEM((ch, tiles + 1, deep, LANES), f32)
    plane = (tiles + 1, deep, LANES)
    *fields_of, parts = pl.pallas_call(
        krylov_kernel,
        out_shape=[field] * 5 + [jax.ShapeDtypeStruct((devices, 1, LANES), f32)],
        in_specs=[ANY] * 4 + [VMEM] * 4,
        out_specs=[VMEM] * 6,
        scratch_shapes=[pltpu.VMEM(plane, i32)] * 2
        + [pltpu.VMEM(plane, f32)] * 5
        + [pltpu.VMEM((MOMENTS * ch, SUBS, LANES), f32), pltpu.SemaphoreType.DMA((4, tiles))],
        compiler_params=pltpu.CompilerParams(vmem_limit_bytes=24 << 20),
        name="krylov",
    )(guidance, initial, labels, dirichlet, from_left, from_right, from_up, from_down)

    parts = lax.all_to_all(parts, ("rows", "cols"), 0, 0)

    result = jax.ShapeDtypeStruct((ch, rows, cols), f32)
    return pl.pallas_call(
        finish_kernel,
        out_shape=[result] * 2,
        in_specs=[VMEM] * 6,
        out_specs=[ANY] * 2,
        scratch_shapes=[pltpu.VMEM((ch, tiles, rows, LANES), f32)] * 2 + [pltpu.SemaphoreType.DMA((2, tiles))],
        compiler_params=pltpu.CompilerParams(vmem_limit_bytes=24 << 20),
        name="finish",
    )(parts, *fields_of)


def solution(mesh):
    in_specs = (
        P(None, "rows", "cols"),
        P(None, "rows", "cols"),
        P("rows", "cols"),
        P("rows", "cols"),
    )
    out_specs = (P(None, "rows", "cols"), P(None, "rows", "cols"))

    def step(*args):
        return tuple(on_device(*args))

    return jax.shard_map(step, mesh=mesh, in_specs=in_specs, out_specs=out_specs, check_vma=False)
```
